32 devices in a mesh: lat: 4 (over y, x), lon: 8 (over z, core).
Axes of the slice: x: 2, y: 2, z: 4, core: 2. Of those that a mesh axis runs over, the one named last changes fastest.
Arguments:
- fine_field: bfloat16 [4, 48, 96, 512], P(None, 'lat', 'lon'), may hold values from -6 to 6
- offsets: int32 [4], replicated, may hold values from 1 to 11, as said below
- fine_prenorm: float32 [512], replicated, may hold values from 0.25 to 1.75
- fine_triple: bfloat16 [512, 1536], replicated, may hold values from -0.25 to 0.25
- fine_bias: float32 [16, 144, 144], replicated, may hold values from -160 to 160
- fine_output: bfloat16 [512, 512], replicated, may hold values from -0.25 to 0.25
- fine_midnorm: float32 [512], replicated, may hold values from 0.25 to 1.75
- fine_expand: bfloat16 [512, 2048], replicated, may hold values from -0.25 to 0.25
- fine_reduce: bfloat16 [2048, 512], replicated, may hold values from -0.125 to 0.125
- merge_gain: float32 [2048], replicated, may hold values from 0.25 to 1.75
- merge_weight: bfloat16 [2048, 1024], replicated, may hold values from -0.125 to 0.125
- coarse_prenorm: float32 [1024], replicated, may hold values from 0.25 to 1.75
- coarse_triple: bfloat16 [1024, 3072], P(None, 'lon'), may hold values from -0.1875 to 0.1875
- coarse_bias: float32 [32, 144, 144], P('lon'), may hold values from -160 to 160
- coarse_output: bfloat16 [1024, 1024], P('lon'), may hold values from -0.1875 to 0.1875
- coarse_midnorm: float32 [1024], replicated, may hold values from 0.25 to 1.75
- coarse_expand: bfloat16 [1024, 4096], P(None, 'lon'), may hold values from -0.1875 to 0.1875
- coarse_reduce: bfloat16 [4096, 1024], P('lon'), may hold values from -0.09375 to 0.09375
- upsample_weight: bfloat16 [1024, 2048], replicated, may hold values from -0.1875 to 0.1875
Outputs:
- blended: bfloat16 [4, 48, 96, 512], P(None, 'lat', 'lon')
- coarse_state: bfloat16 [4, 24, 48, 1024], P(None, 'lat', 'lon')
The draws below stay inside these ranges and needn't reach their ends.
Inputs may be any that keep to these rules, and one draw needn't show every extreme that they name: `offsets`: entries 0 and 2 lie in 1 to 5, entries 1 and 3 in 1 to 11; in every draw entry 0 or entry 2 equals 5, and entry 1 or entry 3 equals 11.
All inputs are finite; a program needn't handle non-finite values.
Results may differ from the reference program's by a relative error of at most 0.024.
Values may be sent and summed in bfloat16 or wider, within the bound.
A program may use at most 128 MiB of HBM per device.

```python
import jax
import jax.numpy as jnp
from jax import lax

C1 = 512
H1 = 16
C2 = 1024
H2 = 32
DEP = 4
WD = 2
WL = 6
WW = 12
WT = 144
FF1 = 2048
FF2 = 4096
HF = 48
WG = 96
WC = 48
N_LON = 8


def pair_score_table(key, head_count):
    base_vals = jnp.clip(jax.random.normal(key, (head_count, WT, WT), jnp.float32), -4.0, 4.0)
    return base_vals


def draw_fine_bias(key, part):
    return pair_score_table(jax.random.fold_in(key, 11), H1)


def draw_coarse_bias(key, part):
    return pair_score_table(jax.random.fold_in(key, 13), H2)


def draw_offsets(key, part):
    key_list = jax.random.split(jax.random.fold_in(key, 3), 4)
    lat_other = jax.random.randint(key_list[0], (), 1, WL)
    lon_other = jax.random.randint(key_list[1], (), 1, WW)
    lat_side = jax.random.randint(key_list[2], (), 0, 2)
    lon_side = jax.random.randint(key_list[3], (), 0, 2)
    lat_most = jnp.full((), WL - 1, jnp.int32)
    lon_most = jnp.full((), WW - 1, jnp.int32)
    fine_lat = jnp.where(lat_side == 0, lat_most, lat_other)
    coarse_lat = jnp.where(lat_side == 0, lat_other, lat_most)
    fine_lon = jnp.where(lon_side == 0, lon_most, lon_other)
    coarse_lon = jnp.where(lon_side == 0, lon_other, lon_most)
    return jnp.stack([fine_lat, fine_lon, coarse_lat, coarse_lon]).astype(jnp.int32)


def shard_levels(rng, extent, shards, low, high):
    factor_of = 1.0
    for position, shards_of in shards:
        heights = jax.random.uniform(jax.random.fold_in(jax.random.fold_in(rng, 6), position), (shards_of,), jnp.float32, low / len(shards), high / len(shards))
        factor_of = factor_of * jnp.repeat(jnp.exp(heights), extent[position] // shards_of).reshape((-1,) + (1,) * (len(extent) - 1 - position))
    return factor_of


def gaussian(rng, shape, scale, limit, cuts=(), kind=jnp.bfloat16):
    level = shard_levels(rng, shape, cuts, -0.22, 0.18) if cuts else 1.0
    drawn = jax.random.normal(rng, shape, jnp.float32) * scale * level
    return jnp.minimum(jnp.maximum(drawn, -limit), limit).astype(kind)


def setup_inputs(seed: int = 0) -> dict:
    arg_keys = jax.random.split(jax.random.key(seed), 20)
    fine_field = gaussian(arg_keys[0], (DEP, HF, WG, C1), 1.0, 6.0, ((1, 4), (2, 8)))
    offsets = draw_offsets(jax.random.fold_in(arg_keys[19], 71), 0)
    fine_prenorm = jnp.clip(1.0 + 0.15 * jax.random.normal(arg_keys[2], (C1,), jnp.float32), 0.25, 1.75)
    fine_triple = gaussian(arg_keys[3], (C1, 3 * C1), C1 ** -0.5, 0.25)
    fine_bias = draw_fine_bias(jax.random.fold_in(arg_keys[19], 71), 0)
    fine_output = gaussian(arg_keys[5], (C1, C1), C1 ** -0.5, 0.25)
    fine_midnorm = jnp.clip(1.0 + 0.15 * jax.random.normal(arg_keys[6], (C1,), jnp.float32), 0.25, 1.75)
    fine_expand = gaussian(arg_keys[7], (C1, FF1), C1 ** -0.5, 0.25)
    fine_reduce = gaussian(arg_keys[8], (FF1, C1), FF1 ** -0.5, 0.125)
    merge_gain = jnp.clip(1.0 + 0.15 * jax.random.normal(arg_keys[9], (4 * C1,), jnp.float32), 0.25, 1.75)
    merge_weight = gaussian(arg_keys[10], (4 * C1, C2), (4 * C1) ** -0.5, 0.125)
    coarse_prenorm = jnp.clip(1.0 + 0.15 * jax.random.normal(arg_keys[11], (C2,), jnp.float32), 0.25, 1.75)
    coarse_triple = gaussian(arg_keys[12], (C2, 3 * C2), C2 ** -0.5, 0.1875, ((1, 8),))
    coarse_bias = draw_coarse_bias(jax.random.fold_in(arg_keys[19], 71), 0)
    coarse_output = gaussian(arg_keys[14], (C2, C2), C2 ** -0.5, 0.1875, ((0, 8),))
    coarse_midnorm = jnp.clip(1.0 + 0.15 * jax.random.normal(arg_keys[15], (C2,), jnp.float32), 0.25, 1.75)
    coarse_expand = gaussian(arg_keys[16], (C2, FF2), C2 ** -0.5, 0.1875, ((1, 8),))
    coarse_reduce = gaussian(arg_keys[17], (FF2, C2), FF2 ** -0.5, 0.09375, ((0, 8),))
    upsample_weight = gaussian(arg_keys[18], (C2, 4 * C1), C2 ** -0.5, 0.1875)
    return dict(fine_field=fine_field, offsets=offsets, fine_prenorm=fine_prenorm, fine_triple=fine_triple, fine_bias=fine_bias, fine_output=fine_output, fine_midnorm=fine_midnorm, fine_expand=fine_expand, fine_reduce=fine_reduce, merge_gain=merge_gain, merge_weight=merge_weight, coarse_prenorm=coarse_prenorm, coarse_triple=coarse_triple, coarse_bias=coarse_bias, coarse_output=coarse_output, coarse_midnorm=coarse_midnorm, coarse_expand=coarse_expand, coarse_reduce=coarse_reduce, upsample_weight=upsample_weight)


epsilon = 1e-05
masked_score = -1e+30

def layer_norm(values, gain_vec):
    values = values.astype(jnp.float32)
    center = lax.optimization_barrier(jnp.mean(values, axis=-1, keepdims=True))
    offset_vals = values - center
    spread = lax.optimization_barrier(jnp.mean(offset_vals * offset_vals, axis=-1, keepdims=True))
    return offset_vals * lax.rsqrt(spread + epsilon) * gain_vec

def to_windows(cells_grid):
    levels, lat_rows, lon_cols, channels = cells_grid.shape
    shaped = cells_grid.reshape(levels // WD, WD, lat_rows // WL, WL, lon_cols // WW, WW, channels)
    shaped = shaped.transpose(0, 2, 4, 1, 3, 5, 6)
    return shaped.reshape(-1, WT, channels)

def from_windows(windows, levels, lat_rows, lon_cols):
    channels = windows.shape[-1]
    shaped = windows.reshape(levels // WD, lat_rows // WL, lon_cols // WW, WD, WL, WW, channels)
    return shaped.transpose(0, 3, 1, 4, 2, 5, 6).reshape(levels, lat_rows, lon_cols, channels)

def window_mix(triples, regions, bias_table):
    count_win = triples.shape[0]
    heads_all = bias_table.shape[0]
    head_dim = triples.shape[-1] // (3 * heads_all)
    parts_all = triples.astype(jnp.float32).reshape(count_win, WT, heads_all, 3, head_dim)
    queries = parts_all[:, :, :, 0]
    keys_all = parts_all[:, :, :, 1]
    values = parts_all[:, :, :, 2]
    scores = jnp.einsum('nihd,njhd->nhij', queries, keys_all) * head_dim ** (-0.5) + bias_table[None]
    allowed = regions[:, :, None] == regions[:, None, :]
    scores = jnp.where(allowed[:, None], scores, masked_score)
    row_top = lax.optimization_barrier(jnp.max(scores, axis=-1, keepdims=True))
    lifted = jnp.exp(scores - row_top)
    weights = (lifted / lax.optimization_barrier(jnp.sum(lifted, axis=-1, keepdims=True))).astype(jnp.bfloat16)
    mixed_out = jnp.einsum('nhij,njhd->nihd', weights.astype(jnp.float32), values)
    return mixed_out.astype(jnp.bfloat16).reshape(count_win, WT, heads_all * head_dim)

def shifted_attention(normed, shift_lat, shift_lon, triple_weight, bias_table):
    levels, lat_rows, lon_cols, channels = normed.shape
    rolled = jnp.roll(normed, (-shift_lat, -shift_lon), axis=(1, 2))
    triples = jnp.dot(rolled.reshape(-1, channels), triple_weight, preferred_element_type=jnp.float32).astype(jnp.bfloat16)
    triples = to_windows(triples.reshape(levels, lat_rows, lon_cols, -1))
    anchor = (jnp.arange(lat_rows, dtype=jnp.int32) + shift_lat) % lat_rows
    regions = jnp.broadcast_to((anchor < shift_lat).astype(jnp.int32)[None, :, None, None], (levels, lat_rows, lon_cols, 1))
    regions = to_windows(regions)[:, :, 0]
    item_count = levels // WD * (lat_rows // WL)
    mixed_out = lax.map(lambda operands: window_mix(operands[0], operands[1], bias_table), (triples.reshape(item_count, -1, WT, triples.shape[-1]), regions.reshape(item_count, -1, WT)))
    mixed_out = from_windows(mixed_out.reshape(-1, WT, mixed_out.shape[-1]), levels, lat_rows, lon_cols)
    return jnp.roll(mixed_out, (shift_lat, shift_lon), axis=(1, 2))

def grouped_sum(operand, weight, groups):
    inner_dim = operand.shape[-1]
    outer_dim = weight.shape[-1]
    split_weight = weight.astype(jnp.float32).reshape(groups, inner_dim // groups, outer_dim)

    def one_block(token_block):
        shaped = token_block.astype(jnp.float32).reshape(token_block.shape[0], groups, inner_dim // groups)
        partials = jnp.einsum('tgk,gkn->tgn', shaped, split_weight).astype(jnp.bfloat16)
        return lax.optimization_barrier(jnp.sum(partials.astype(jnp.float32), axis=1))
    blocks = operand.reshape(-1, WC, inner_dim)
    return lax.map(one_block, blocks).reshape(-1, outer_dim)

def reference(fine_field, offsets, fine_prenorm, fine_triple, fine_bias, fine_output, fine_midnorm, fine_expand, fine_reduce, merge_gain, merge_weight, coarse_prenorm, coarse_triple, coarse_bias, coarse_output, coarse_midnorm, coarse_expand, coarse_reduce, upsample_weight):
    levels, lat_rows, lon_cols, channels = fine_field.shape
    normed = layer_norm(fine_field, fine_prenorm).astype(jnp.bfloat16)
    mixed_out = shifted_attention(normed, offsets[0], offsets[1], fine_triple, fine_bias)
    attended = (fine_field.astype(jnp.float32).reshape(-1, channels) + jnp.dot(mixed_out.reshape(-1, channels), fine_output, preferred_element_type=jnp.float32)).astype(jnp.bfloat16)
    hidden = jax.nn.gelu(jnp.dot(layer_norm(attended, fine_midnorm).astype(jnp.bfloat16), fine_expand, preferred_element_type=jnp.float32)).astype(jnp.bfloat16)
    fine_state = (attended.astype(jnp.float32) + jnp.dot(hidden, fine_reduce, preferred_element_type=jnp.float32)).astype(jnp.bfloat16)
    fine_state = fine_state.reshape(levels, lat_rows, lon_cols, channels)
    half_rows = lat_rows // 2
    half_cols = lon_cols // 2
    merged = fine_state.reshape(levels, half_rows, 2, half_cols, 2, channels).transpose(0, 1, 3, 4, 2, 5)
    merged = merged.reshape(-1, 4 * channels)
    coarse_in = jnp.dot(layer_norm(merged, merge_gain).astype(jnp.bfloat16), merge_weight, preferred_element_type=jnp.float32).astype(jnp.bfloat16)
    wide_channels = coarse_in.shape[-1]
    normed2 = layer_norm(coarse_in, coarse_prenorm).astype(jnp.bfloat16).reshape(levels, half_rows, half_cols, wide_channels)
    mixed2 = shifted_attention(normed2, offsets[2], offsets[3], coarse_triple, coarse_bias)
    coarse_mid = (coarse_in.astype(jnp.float32) + grouped_sum(mixed2.reshape(-1, wide_channels), coarse_output, N_LON)).astype(jnp.bfloat16)
    hidden2 = jax.nn.gelu(jnp.dot(layer_norm(coarse_mid, coarse_midnorm).astype(jnp.bfloat16), coarse_expand, preferred_element_type=jnp.float32)).astype(jnp.bfloat16)
    coarse_state = (coarse_mid.astype(jnp.float32) + grouped_sum(hidden2, coarse_reduce, N_LON)).astype(jnp.bfloat16)
    expanded = jnp.dot(coarse_state, upsample_weight, preferred_element_type=jnp.float32).reshape(levels, half_rows, half_cols, 2, 2, channels)
    expanded = expanded.transpose(0, 1, 4, 2, 3, 5).reshape(levels, lat_rows, lon_cols, channels)
    blended = (fine_state.astype(jnp.float32) + expanded).astype(jnp.bfloat16)
    return (blended, coarse_state.reshape(levels, half_rows, half_cols, wide_channels))
```

```python
import functools

import jax
import jax.numpy as jnp
from jax import lax
from jax.experimental import pallas as pl
from jax.experimental.pallas import tpu as pltpu
from jax.sharding import PartitionSpec as P

WD = 2
WL = 6
WW = 12
WT = 144
HALF = WL * WW

epsilon = 1e-05
masked_score = -1e30
BF = jnp.bfloat16
F32 = jnp.float32


def layer_norm(values, gain_vec):
    values = values.astype(F32)
    center = jnp.mean(values, axis=-1, keepdims=True)
    offset_vals = values - center
    spread = jnp.mean(offset_vals * offset_vals, axis=-1, keepdims=True)
    return (offset_vals * lax.rsqrt(spread + epsilon) * gain_vec).astype(BF)


def dot32(left, right):
    return jnp.dot(left, right, preferred_element_type=F32)


def pick(source_rows, table):
    columns = jnp.arange(table.shape[0], dtype=jnp.int32)
    chosen = (source_rows[:, None] == columns[None, :]).astype(BF)
    return dot32(chosen, table).astype(BF)


def moved(block, axes, deltas):
    sizes = [lax.axis_size(a) for a in axes]
    pairs = []
    if len(axes) == 1:
        n = sizes[0]
        pairs = [((i - deltas[0]) % n, i) for i in range(n)]
        return lax.ppermute(block, axes[0], pairs)
    n, m = sizes
    for i in range(n):
        for j in range(m):
            origin = ((i - deltas[0]) % n) * m + (j - deltas[1]) % m
            pairs.append((origin, i * m + j))
    return lax.ppermute(block, axes, pairs)


def attend(triples, heads_all, head_dim, bias_ref, place_mask, write):
    group = 4 if heads_all % 4 == 0 else heads_all
    lanes = group * head_dim
    width = 3 * lanes
    row_id = lax.broadcasted_iota(jnp.int32, (width, width), 0)
    col_id = lax.broadcasted_iota(jnp.int32, (width, width), 1)
    kind = col_id // lanes
    head = (col_id % lanes) // head_dim
    origin = head * (3 * head_dim) + kind * head_dim + col_id % head_dim
    order = (row_id == origin).astype(F32).astype(BF)
    lane = lax.broadcasted_iota(jnp.int32, (WT, lanes), 1) // head_dim
    for g in range(heads_all // group):
        part = dot32(triples[:, g * width : (g + 1) * width], order)
        queries = part[:, :lanes]
        keys_all = part[:, lanes : 2 * lanes].astype(BF)
        values = part[:, 2 * lanes :].astype(BF)
        total = None
        for h in range(group):
            mine = jnp.where(lane == h, queries, 0.0).astype(BF)
            scores = lax.dot_general(
                mine, keys_all, (((1,), (1,)), ((), ())), preferred_element_type=F32
            )
            scores = scores * head_dim ** (-0.5) + bias_ref[g * group + h] + place_mask
            top = jnp.max(scores, axis=-1, keepdims=True)
            lifted = jnp.exp(scores - top)
            weight_sum = jnp.sum(lifted, axis=-1, keepdims=True)
            mixed = dot32(lifted.astype(BF), values) / weight_sum
            mixed = jnp.where(lane == h, mixed, 0.0)
            total = mixed if total is None else total + mixed
        write(g * lanes, lanes, total.astype(BF))


def window_mask(limit):
    row = (lax.broadcasted_iota(jnp.int32, (WT, WT), 0) // WW) % WL
    col = (lax.broadcasted_iota(jnp.int32, (WT, WT), 1) // WW) % WL
    row_in = (row >= limit).astype(jnp.int32)
    col_in = (col >= limit).astype(jnp.int32)
    return jnp.where(row_in == col_in, 0.0, masked_score)


def attention_kernel(head_dim, heads_all, projected, limit_ref, x_ref, *refs):
    if projected:
        bias_ref, out_ref = refs
        triples = x_ref[...]
    else:
        gain_ref, weight_ref, bias_ref, out_ref = refs
        triples = dot32(layer_norm(x_ref[...], gain_ref[...]), weight_ref[...]).astype(BF)

    def write(start, size, value):
        out_ref[:, start : start + size] = value

    attend(
        triples,
        heads_all,
        head_dim,
        bias_ref,
        window_mask(limit_ref[pl.program_id(0)]),
        write,
    )


def whole_block(array):
    zeros = (0,) * array.ndim
    return pl.BlockSpec(array.shape, lambda i: zeros)


def rows_block(array, rows):
    return pl.BlockSpec((rows, array.shape[1]), lambda i: (i, 0))


def attention(limits, rows, bias_table, head_dim, gain_vec=None, weight=None):
    heads_all = bias_table.shape[0]
    count = rows.shape[0] // WT
    extra = [] if weight is None else [gain_vec[None], weight]
    extra = extra + [bias_table]
    wide = heads_all * head_dim
    return pl.pallas_call(
        functools.partial(attention_kernel, head_dim, heads_all, weight is None),
        out_shape=jax.ShapeDtypeStruct((rows.shape[0], wide), BF),
        grid=(count,),
        in_specs=[pl.BlockSpec(memory_space=pltpu.SMEM), rows_block(rows, WT)]
        + [whole_block(e) for e in extra],
        out_specs=pl.BlockSpec((WT, wide), lambda i: (i, 0)),
        compiler_params=pltpu.CompilerParams(vmem_limit_bytes=40 << 20),
    )(limits, rows, *extra)


def tail_kernel(m_ref, x_ref, wo_ref, g_ref, we_ref, wr_ref, out_ref):
    attended = (x_ref[...].astype(F32) + dot32(m_ref[...], wo_ref[...])).astype(BF)
    hidden = jax.nn.gelu(dot32(layer_norm(attended, g_ref[...]), we_ref[...])).astype(BF)
    out_ref[...] = (attended.astype(F32) + dot32(hidden, wr_ref[...])).astype(BF)


def fine_tail(mixed, field, w_out, gain_vec, w_expand, w_reduce, rows):
    gain_vec = gain_vec[None]
    return pl.pallas_call(
        tail_kernel,
        out_shape=jax.ShapeDtypeStruct(field.shape, BF),
        grid=(field.shape[0] // rows,),
        in_specs=[rows_block(mixed, rows), rows_block(field, rows)]
        + [whole_block(e) for e in (w_out, gain_vec, w_expand, w_reduce)],
        out_specs=rows_block(field, rows),
        compiler_params=pltpu.CompilerParams(vmem_limit_bytes=40 << 20),
    )(mixed, field, w_out, gain_vec, w_expand, w_reduce)


def feed_kernel(x_ref, g_ref, we_ref, wr_ref, out_ref):
    hidden = jax.nn.gelu(dot32(layer_norm(x_ref[...], g_ref[...]), we_ref[...])).astype(BF)
    out_ref[...] = dot32(hidden, wr_ref[...]).astype(BF)


def feed(rows_in, gain_vec, w_expand, w_reduce, rows):
    gain_vec = gain_vec[None]
    return pl.pallas_call(
        feed_kernel,
        out_shape=jax.ShapeDtypeStruct(rows_in.shape, BF),
        grid=(rows_in.shape[0] // rows,),
        in_specs=[rows_block(rows_in, rows)]
        + [whole_block(e) for e in (gain_vec, w_expand, w_reduce)],
        out_specs=rows_block(rows_in, rows),
        compiler_params=pltpu.CompilerParams(vmem_limit_bytes=40 << 20),
    )(rows_in, gain_vec, w_expand, w_reduce)


def norm_dot_kernel(x_ref, g_ref, w_ref, out_ref):
    out_ref[...] = dot32(layer_norm(x_ref[...], g_ref[...]), w_ref[...]).astype(BF)


def norm_dot(rows_in, gain_vec, weight, rows):
    gain_vec = gain_vec[None]
    return pl.pallas_call(
        norm_dot_kernel,
        out_shape=jax.ShapeDtypeStruct((rows_in.shape[0], weight.shape[1]), BF),
        grid=(rows_in.shape[0] // rows,),
        in_specs=[rows_block(rows_in, rows)] + [whole_block(e) for e in (gain_vec, weight)],
        out_specs=pl.BlockSpec((rows, weight.shape[1]), lambda i: (i, 0)),
        compiler_params=pltpu.CompilerParams(vmem_limit_bytes=40 << 20),
    )(rows_in, gain_vec, weight)


def window_cells(total, rows, cols):
    n = jnp.arange(total, dtype=jnp.int32)
    w, place = n // WT, n % WT
    wc = w % (cols // WW)
    wl = (w // (cols // WW)) % (rows // WL)
    pd = w // ((cols // WW) * (rows // WL))
    return (
        pd * WD + place // HALF,
        wl * WL + (place // WW) % WL,
        wc * WW + place % WW,
    )


def window_place(p, i, j, rows, cols):
    w = ((p // WD) * (rows // WL) + i // WL) * (cols // WW) + j // WW
    return w * WT + (p % WD) * HALF + (i % WL) * WW + j % WW


def body(
    fine_field,
    offsets,
    fine_prenorm,
    fine_triple,
    fine_bias,
    fine_output,
    fine_midnorm,
    fine_expand,
    fine_reduce,
    merge_gain,
    merge_weight,
    coarse_prenorm,
    coarse_triple,
    coarse_bias,
    coarse_output,
    coarse_midnorm,
    coarse_expand,
    coarse_reduce,
    upsample_weight,
):
    levels, lat_rows, lon_cols, channels = fine_field.shape
    lat_count = lax.axis_size("lat")
    group_count = lax.axis_size("lon")
    lat_index = lax.axis_index("lat")
    s0, s1, s2, s3 = offsets[0], offsets[1], offsets[2], offsets[3]
    halo = WL - 1
    full_output = lax.all_gather(coarse_output, "lon", axis=0, tiled=True)

    cells = levels * lat_rows * lon_cols
    field = fine_field.reshape(cells, channels)
    strip = fine_field[:, :halo].reshape(-1, channels)
    strip_rows = strip.shape[0]
    extended = jnp.concatenate(
        [
            field,
            moved(field, ("lon",), (-1,)),
            moved(strip, ("lat",), (-1,)),
            moved(strip, ("lat", "lon"), (-1, -1)),
        ],
        axis=0,
    )
    p, i, j = window_cells(cells, lat_rows, lon_cols)
    i, j = i + s0, j + s1
    below, beside = i >= lat_rows, j >= lon_cols
    jj = jnp.where(beside, j - lon_cols, j)
    here = (p * lat_rows + i) * lon_cols + jj + jnp.where(beside, cells, 0)
    there = (
        2 * cells
        + (p * halo + i - lat_rows) * lon_cols
        + jj
        + jnp.where(beside, strip_rows, 0)
    )
    framed = pick(jnp.where(below, there, here), extended)
    win_rows = (jnp.arange(cells // WT, dtype=jnp.int32) // (lon_cols // WW)) % (lat_rows // WL)
    limits = lat_rows * lat_count - s0 - lat_index * lat_rows - win_rows * WL
    head_dim = channels // fine_bias.shape[0]
    mixed = attention(limits, framed, fine_bias, head_dim, fine_prenorm, fine_triple)

    u = jnp.arange(strip_rows, dtype=jnp.int32)
    up = u // (halo * lon_cols)
    ui = (u // lon_cols) % halo + lat_rows - halo
    mixed_strip = pick(window_place(up, ui, u % lon_cols, lat_rows, lon_cols), mixed)
    returned = jnp.concatenate(
        [
            mixed,
            moved(mixed, ("lon",), (1,)),
            moved(mixed_strip, ("lat",), (1,)),
            moved(mixed_strip, ("lat", "lon"), (1, 1)),
        ],
        axis=0,
    )
    half_rows = lat_rows // 2
    half_cols = lon_cols // 2
    few = cells // 4
    n = jnp.arange(cells, dtype=jnp.int32)
    block, cell = n // few, n % few
    c = cell % half_cols
    p = (cell // half_cols) % levels
    i = (cell // (half_cols * levels)) * 2 + block % 2
    j = c * 2 + block // 2
    ordered = pick((p * lat_rows + i) * lon_cols + j, field)
    fi, fj = i - s0, j - s1
    west = fj < 0
    fj = jnp.where(west, fj + lon_cols, fj)
    here = window_place(p, jnp.maximum(fi, 0), fj, lat_rows, lon_cols) + jnp.where(west, cells, 0)
    there = (
        2 * cells
        + (p * halo + fi + halo) * lon_cols
        + fj
        + jnp.where(west, strip_rows, 0)
    )
    mixed = pick(jnp.where(fi < 0, there, here), returned)
    fine_state = fine_tail(
        mixed, ordered, fine_output, fine_midnorm, fine_expand, fine_reduce, few
    )
    merged = jnp.concatenate([fine_state[k * few : (k + 1) * few] for k in range(4)], axis=1)
    coarse_in = norm_dot(merged, merge_gain, merge_weight, few)

    wide = coarse_in.shape[1]
    band = few * group_count
    band_cols = half_cols * group_count
    band_cells = lax.all_gather(coarse_in, "lon", axis=0, tiled=True)
    triples = norm_dot(band_cells, coarse_prenorm, coarse_triple, few)
    triple_width = triples.shape[1]
    per_row = levels * half_cols
    strip2 = triples.reshape(group_count, few, triple_width)[:, : halo * per_row]
    strip2 = strip2.reshape(-1, triple_width)
    extended2 = jnp.concatenate([triples, moved(strip2, ("lat",), (-1,))], axis=0)
    p, r, col = window_cells(band, half_rows, band_cols)
    r = r + s2
    col = (col + s3) % band_cols
    owner, c = col // half_cols, col % half_cols
    here = owner * few + r * per_row + p * half_cols + c
    there = band + owner * (halo * per_row) + (r - half_rows) * per_row + p * half_cols + c
    framed2 = pick(jnp.where(r >= half_rows, there, here), extended2)
    win_rows2 = (jnp.arange(band // WT, dtype=jnp.int32) // (band_cols // WW)) % (half_rows // WL)
    limits2 = half_rows * lat_count - s2 - lat_index * half_rows - win_rows2 * WL
    head_dim2 = triple_width // (3 * coarse_bias.shape[0])
    mixed2 = attention(limits2, framed2, coarse_bias, head_dim2)
    returned2 = jnp.concatenate([mixed2, moved(mixed2, ("lat",), (1,))], axis=0)
    n = jnp.arange(band, dtype=jnp.int32)
    owner, cell = n // few, n % few
    c = cell % half_cols
    p = (cell // half_cols) % levels
    fr = cell // per_row - s2
    col = (owner * half_cols + c - s3 + band_cols) % band_cols
    north = fr < 0
    fr = jnp.where(north, fr + half_rows, fr)
    source = window_place(p, fr, col, half_rows, band_cols) + jnp.where(north, band, 0)
    mixed2 = pick(source, returned2)
    mixed_width = mixed2.shape[1]
    parts = lax.all_to_all(
        mixed2.reshape(group_count, few, mixed_width), "lon", split_axis=0, concat_axis=0, tiled=True
    )
    grouped = jnp.concatenate([parts[g] for g in range(group_count)], axis=1)
    coarse_mid = (coarse_in.astype(F32) + dot32(grouped, full_output)).astype(BF)
    mid_band = lax.all_gather(coarse_mid, "lon", axis=0, tiled=True)
    product = feed(mid_band, coarse_midnorm, coarse_expand, coarse_reduce, few)
    feed_sum = lax.psum_scatter(product, "lon", scatter_dimension=0, tiled=True).astype(F32)
    coarse_state = (coarse_mid.astype(F32) + feed_sum).astype(BF)
    expanded = dot32(coarse_state, upsample_weight)
    spread = jnp.concatenate(
        [expanded[:, k * channels : (k + 1) * channels] for k in range(4)], axis=0
    )
    blended = (fine_state.astype(F32) + spread).astype(BF)
    n = jnp.arange(cells, dtype=jnp.int32)
    p = n // (lat_rows * lon_cols)
    i = (n // lon_cols) % lat_rows
    j = n % lon_cols
    source = (
        ((j % 2) * 2 + i % 2) * few + (i // 2) * per_row + p * half_cols + j // 2
    )
    blended = pick(source, blended).reshape(fine_field.shape)
    n = jnp.arange(few, dtype=jnp.int32)
    p = n // (half_rows * half_cols)
    r = (n // half_cols) % half_rows
    state = pick(r * per_row + p * half_cols + n % half_cols, coarse_state)
    return (blended, state.reshape(levels, half_rows, half_cols, wide))


def solution(mesh):
    placed = (
        P(None, "lat", "lon", None),
        P(),
        P(),
        P(),
        P(),
        P(),
        P(),
        P(),
        P(),
        P(),
        P(),
        P(),
        P(None, "lon"),
        P("lon", None, None),
        P("lon", None),
        P(),
        P(None, "lon"),
        P("lon", None),
        P(),
    )
    return jax.shard_map(
        body,
        mesh=mesh,
        in_specs=placed,
        out_specs=(P(None, "lat", "lon", None), P(None, "lat", "lon", None)),
        check_vma=False,
    )
```
